32 devices in a mesh: feat: 16 (over z, y, x), dp: 2 (over core).
Axes of the slice: x: 2, y: 2, z: 4, core: 2. Of those that a mesh axis runs over, the one named last changes fastest.
Arguments:
- activations: bfloat16 [1024, 16384], P('dp', 'feat')
- norm_gain: float32 [16384], replicated, may hold values from 0.5 to 1.5
- weights: float32 [1024, 16384], P('dp', 'feat'), may hold values from -6 to 6
- inverse_factor: float32 [128, 16384], P(None, 'feat'), as said below
- grid_scales: float32 [1024], P('dp'), may hold values from 0.5 to 2
Outputs:
- hessian: float32 [16384, 16384], P('dp', 'feat')
- updated_weights: float32 [1024, 16384], P('dp', 'feat')
The draws below stay inside these ranges and needn't reach their ends.
Inputs may be any that keep to these rules, and one draw needn't show every extreme that they name: `inverse_factor`: in the first 128 columns, the diagonal lies in 1 to 2 and entries below it are zero.
All inputs are finite; a program needn't handle non-finite values.
Results may differ from the reference program's by a relative error of at most 0.012.
Values may be sent and summed in bfloat16 or wider, within the bound.
No kernel may reach another device: no remote copies, remote signals or barrier semaphores. Data moves between devices by JAX's collectives and lax.ppermute only.
A program may use at most 128 MiB of HBM per device.

```python
import math
import jax
import jax.numpy as jnp
from jax import lax

D = 16384
PANEL = 128
TOK_DEV = 512
TOKENS = 1024
OUT = 1024
N_FEAT = 16
N_DP = 2


def draw_activations(key, part):
    noise_key, row_key, column_key = jax.random.split(jax.random.fold_in(key, 11), 3)
    noise = jax.random.normal(noise_key, (TOKENS, D), jnp.float32)
    row_scale = jnp.exp(jax.random.uniform(row_key, (TOKENS, 1), jnp.float32, 0.0, math.log(10.0)))
    rising = 1.0 + 2.0 * jnp.arange(D, dtype=jnp.float32) / (D - 1)
    column_scale = rising[None, :] * jnp.exp(jax.random.uniform(column_key, (1, D), jnp.float32, -0.7, 0.7))
    return (noise * row_scale * column_scale).astype(jnp.bfloat16)


def draw_inverse_factor(key, part):
    noise_key, pivot_key = jax.random.split(jax.random.fold_in(key, 23), 2)
    spread = jnp.clip(0.3 * jax.random.normal(noise_key, (PANEL, D), jnp.float32), -1.2, 1.2)
    pivots = 1.0 + jax.random.uniform(pivot_key, (PANEL, D), jnp.float32)
    row_ids = jnp.arange(PANEL)[:, None]
    column_ids = jnp.arange(D)[None, :]
    result = jnp.where(row_ids == column_ids, pivots, spread)
    result = jnp.where((column_ids < PANEL) & (column_ids < row_ids), jnp.zeros_like(result), result)
    return result.astype(jnp.float32)


def shard_levels(rng, extent, shards, least, largest):
    factor_of, own = 1.0, jax.random.fold_in(rng, 6)
    for position, parts in shards:
        draws = jnp.exp(jax.random.uniform(jax.random.fold_in(own, position), (parts,), jnp.float32, least / len(shards), largest / len(shards)))
        factor_of = factor_of * jnp.repeat(draws, extent[position] // parts).reshape([-1 if axis == position else 1 for axis in range(len(extent))])
    return factor_of


def scatter_about(stream_key, dims, width, limit, cuts=(), held_as=jnp.bfloat16):
    drawn = width * jax.random.normal(stream_key, dims, jnp.float32)
    if cuts:
        drawn = drawn * shard_levels(stream_key, dims, cuts, -0.22, 0.18)
    return jnp.clip(drawn, -limit, limit).astype(held_as)


def setup_inputs(seed: int = 0) -> dict:
    seeds = jax.random.split(jax.random.key(seed), 6)
    activations = draw_activations(jax.random.fold_in(seeds[5], 71), 0)
    norm_gain = jnp.clip(1.0 + 0.1 * jax.random.normal(seeds[1], (D,), jnp.float32), 0.5, 1.5)
    weights = scatter_about(seeds[2], (OUT, D), 1.0, 6.0, ((0, 2), (1, 16)), jnp.float32)
    inverse_factor = draw_inverse_factor(jax.random.fold_in(seeds[5], 71), 0)
    grid_scales = jnp.clip(jnp.exp(math.log(2.0) - 1.3862944 * jax.random.uniform(seeds[4], (OUT,), jnp.float32) ** shard_levels(seeds[4], (OUT,), ((0, 2),), -0.2, 0.2)), 0.5, 2.0)
    return dict(activations=activations, norm_gain=norm_gain, weights=weights, inverse_factor=inverse_factor, grid_scales=grid_scales)


norm_epsilon = 1e-05
full_turn = 2.0 * math.pi

def quantize_panel(panel_rows, factor_block, grid_scales):
    panel_width = factor_block.shape[0]
    diagonal_entries = jnp.diagonal(factor_block)
    positions = jnp.arange(panel_width)

    def advance(index, carry):
        working, quantized, residue = carry
        current = lax.dynamic_index_in_dim(working, index, 0, keepdims=False)
        grid_ratio = current / grid_scales
        dequantized = grid_scales * (grid_ratio - jnp.sin(full_turn * grid_ratio) / full_turn)
        pivot_entry = lax.dynamic_index_in_dim(diagonal_entries, index, 0, keepdims=False)
        scaled_error = (current - dequantized) / pivot_entry
        factor_row = lax.dynamic_index_in_dim(factor_block, index, 0, keepdims=False)
        factor_row = jnp.where(positions > index, factor_row, jnp.zeros_like(factor_row))
        working = working - factor_row[:, None] * scaled_error[None, :]
        quantized = lax.dynamic_update_index_in_dim(quantized, dequantized, index, 0)
        residue = lax.dynamic_update_index_in_dim(residue, scaled_error, index, 0)
        return (working, quantized, residue)
    blank = jnp.zeros_like(panel_rows)
    final = lax.fori_loop(0, panel_width, advance, (panel_rows, blank, blank))
    return (final[1], final[2])

def reference(activations, norm_gain, weights, inverse_factor, grid_scales):
    widened = activations.astype(jnp.float32)
    row_squares = lax.optimization_barrier(jnp.sum(widened * widened, axis=1, keepdims=True))
    normed = (widened * lax.rsqrt(row_squares / D + norm_epsilon) * norm_gain[None, :]).astype(jnp.bfloat16)
    block_width = D // N_FEAT
    grouped = normed.reshape(N_DP, TOK_DEV, D)

    def column_block(block_index):
        start = (block_index * block_width).astype(jnp.int32)
        columns = lax.dynamic_slice_in_dim(normed, start, block_width, 1).reshape(N_DP, TOK_DEV, block_width)

        def group_term(running, inputs):
            group_rows, group_columns = inputs
            term = jnp.dot(group_rows.T, group_columns, preferred_element_type=jnp.float32) / TOKENS
            rounded = lax.optimization_barrier(term.astype(jnp.bfloat16))
            return (running + rounded.astype(jnp.float32), None)
        total, unused = lax.scan(group_term, jnp.zeros((D, block_width), jnp.float32), (grouped, columns))
        return total
    stacked = lax.map(column_block, jnp.arange(N_FEAT).astype(jnp.int32))
    hessian = jnp.transpose(stacked, (1, 0, 2)).reshape(D, D)
    panel_rows = weights[:, :PANEL].T
    factor_block = inverse_factor[:, :PANEL]
    quantized, residue = quantize_panel(panel_rows, factor_block, grid_scales)
    shift_terms = lax.dot_general(residue, inverse_factor, (((0,), (0,)), ((), ())), precision=lax.Precision.HIGHEST, preferred_element_type=jnp.float32)
    updated_weights = weights - shift_terms
    updated_weights = updated_weights.at[:, :PANEL].set(quantized.T)
    return (hessian, updated_weights)
```

```python
import functools

import jax
import jax.numpy as jnp
from jax import lax
from jax.experimental import pallas as pl
from jax.experimental.pallas import tpu as pltpu
from jax.sharding import PartitionSpec as P

norm_epsilon = 1e-05
sine_terms = (
    0.9999999945157819,
    -6.579735444308534,
    12.987843048997036,
    -12.207431000310573,
    6.687080392696814,
    -2.366412636519861,
    0.509246668107693,
)
axes = ("feat", "dp")


def bits_below(count):
    return [1 << n for n in range(count.bit_length() - 1)]


def permute(value, feat_mask, dp_mask=0, sends=lambda f, d: True):
    feats, parts = lax.axis_size("feat"), lax.axis_size("dp")
    pairs = [
        (f * parts + d, (f ^ feat_mask) * parts + (d ^ dp_mask))
        for f in range(feats)
        for d in range(parts)
        if sends(f, d)
    ]
    return lax.ppermute(value, axes, pairs)


def panel_kernel(weights_ref, factor_ref, scales_ref, quantized_ref, residue_ref, work, kept, errors):
    group = 8
    width = factor_ref.shape[0]
    work[...] = weights_ref[...].T
    scales = jnp.broadcast_to(scales_ref[...], (group, scales_ref.shape[1]))
    inverse_scales = 1.0 / scales
    rows_down = lax.broadcasted_iota(jnp.int32, (group, 1), 0)
    square = lax.broadcasted_iota(jnp.int32, (group, group), 0) == lax.broadcasted_iota(
        jnp.int32, (group, group), 1
    )
    lanes = lax.broadcasted_iota(jnp.int32, (group, width), 1)

    def block(number, carry):
        start = pl.multiple_of(number * group, group)
        factor_rows = factor_ref[pl.ds(start, group), :]
        turned = pltpu.roll(factor_rows, lax.rem(width - start, width), 1).T[:group, :]
        pivots = 1.0 / jnp.where(square, turned, 1.0)
        tile = work[pl.ds(start, group), :]
        residues = jnp.zeros_like(tile)
        quantized = jnp.zeros_like(tile)
        for i in range(group):
            row = jnp.broadcast_to(tile[i : i + 1, :], tile.shape)
            ratio = row * inverse_scales
            turn = ratio - jnp.round(ratio)
            squared = turn * turn
            total = jnp.full_like(squared, sine_terms[-1])
            for term in sine_terms[-2::-1]:
                total = total * squared + term
            error = scales * (turn * total)
            scaled = error * pivots[i : i + 1, i : i + 1]
            here = rows_down == i
            quantized = jnp.where(here, row - error, quantized)
            residues = jnp.where(here, scaled, residues)
            column = jnp.where(rows_down > i, turned[:, i : i + 1], 0.0)
            tile = tile - column * scaled
        kept[pl.ds(start, group), :] = quantized
        errors[pl.ds(start, group), :] = residues
        later = jnp.where(lanes >= start + group, factor_rows, 0.0)
        work[...] = work[...] - lax.dot_general(
            later,
            residues,
            (((0,), (0,)), ((), ())),
            precision=lax.Precision.HIGHEST,
            preferred_element_type=jnp.float32,
        )
        return carry

    lax.fori_loop(0, width // group, block, 0)
    quantized_ref[...] = kept[...].T
    residue_ref[...] = errors[...].astype(residue_ref.dtype)


def quantize_panel(weights, inverse_factor, grid_scales):
    rows, width = weights.shape[0], inverse_factor.shape[0]
    return pl.pallas_call(
        panel_kernel,
        grid=(1,),
        out_shape=(
            jax.ShapeDtypeStruct((rows, width), jnp.float32),
            jax.ShapeDtypeStruct((width, rows), jnp.bfloat16),
        ),
        in_specs=[
            pl.BlockSpec((rows, width), lambda i: (0, 0)),
            pl.BlockSpec((width, width), lambda i: (0, 0)),
            pl.BlockSpec((1, rows), lambda i: (0, 0)),
        ],
        out_specs=(
            pl.BlockSpec((rows, width), lambda i: (0, 0)),
            pl.BlockSpec((width, rows), lambda i: (0, 0)),
        ),
        scratch_shapes=[pltpu.VMEM((width, rows), jnp.float32)] * 3,
        compiler_params=pltpu.CompilerParams(vmem_limit_bytes=16 << 20),
        cost_estimate=pl.CostEstimate(
            flops=60 * rows * width, bytes_accessed=12 * rows * width, transcendentals=0
        ),
        name="panel",
    )(weights, inverse_factor, grid_scales[None, :])


def gram_kernel(place_ref, own_ref, sent_ref, scaled_ref, gain_ref, *rest):
    out_ref = rest[-1]
    picked = jnp.where(place_ref[1] == 1, own_ref[...], sent_ref[...])
    product = lax.dot_general(
        picked, scaled_ref[...], (((0,), (0,)), ((), ())), preferred_element_type=jnp.float32
    )
    lanes = 128
    gain = jnp.broadcast_to(gain_ref[0], (lanes, gain_ref.shape[2])).T
    for start in range(0, out_ref.shape[1], lanes):
        out_ref[:, start : start + lanes] = product[:, start : start + lanes] * gain


def gram_rows(place, own, sent, scaled, gain, hessian, height):
    tokens, columns = own.shape
    width = scaled.shape[1]
    tile = min(256, columns)
    steps = columns // tile
    operands = [place, own, sent, scaled, gain]
    in_specs = [
        pl.BlockSpec((tokens, tile), lambda i, place: (0, i * place[1])),
        pl.BlockSpec((tokens, tile), lambda i, place: (0, i * (1 - place[1]))),
        pl.BlockSpec((tokens, width), lambda i, place: (0, 0), pipeline_mode=pl.Buffered(1)),
        pl.BlockSpec((1, 1, tile), lambda i, place: (place[2] * steps + i, 0, 0)),
    ]
    aliases = {}
    if hessian is not None:
        aliases = {len(operands): 0}
        operands.append(hessian)
        in_specs.append(pl.BlockSpec(memory_space=pl.ANY))
    return pl.pallas_call(
        gram_kernel,
        grid_spec=pltpu.PrefetchScalarGridSpec(
            num_scalar_prefetch=1,
            grid=(steps,),
            in_specs=in_specs,
            out_specs=pl.BlockSpec((tile, width), lambda i, place: (place[0] * steps + i, 0)),
        ),
        out_shape=jax.ShapeDtypeStruct((height, width), jnp.float32),
        input_output_aliases=aliases,
        compiler_params=pltpu.CompilerParams(vmem_limit_bytes=32 << 20),
        cost_estimate=pl.CostEstimate(
            flops=2 * tokens * columns * width,
            bytes_accessed=2 * tokens * (columns + width) + 4 * columns * width,
            transcendentals=0,
        ),
        name="gram",
    )(*operands)


def body(activations, norm_gain, weights, inverse_factor, grid_scales):
    row_count, shard_width = activations.shape
    feats, parts = lax.axis_size("feat"), lax.axis_size("dp")
    token_total = row_count * parts
    full_width = shard_width * feats
    share = feats // parts
    feat, part = lax.axis_index("feat"), lax.axis_index("dp")
    own_start = feat * shard_width
    near = bits_below(share)

    def inside(f, d):
        return f // share == d

    def outside(f, d):
        return f // share != d

    token_sets = [activations] + [permute(activations, 0, m) for m in range(1, parts)]

    widened = activations.astype(jnp.float32)
    row_squares = jnp.sum(widened * widened, axis=1)
    for mask in bits_below(feats):
        row_squares = row_squares + permute(row_squares, mask)
    inverse_rms = lax.rsqrt(row_squares / full_width + norm_epsilon)
    all_rms = jnp.concatenate([inverse_rms] + [permute(inverse_rms, 0, m) for m in range(1, parts)])
    own_gain = lax.dynamic_slice_in_dim(norm_gain, own_start, shard_width, 0)

    colours = 2 if len(near) > 1 else 1
    orders = [near]
    if colours == 2:
        orders = [[near[0]] + near[2:] + [near[1]], [near[1]] + near[2:] + [near[0]]]
    chunk_width = shard_width // colours
    chunks = [
        jnp.concatenate([t[:, c * chunk_width : (c + 1) * chunk_width] for t in token_sets], axis=0)
        for c in range(colours)
    ]
    scaled = jnp.concatenate(token_sets, axis=0).astype(jnp.float32)
    scaled = (scaled * all_rms[:, None] * (all_rms[:, None] * own_gain[None, :])).astype(jnp.bfloat16)

    panel_width = inverse_factor.shape[0]
    quantized, residue = quantize_panel(weights, inverse_factor, grid_scales)
    residue = jnp.where(feat == 0, residue, 0).astype(residue.dtype)

    inner = [{0: c} for c in chunks]
    outer = []
    for chunk in chunks:
        arrived = None
        for m in range(1, parts):
            got = permute(chunk, m * share, 0, inside)
            arrived = got if arrived is None else arrived + got
        outer.append({0: arrived})
    for held, sends in ((inner, inside), (outer, outside)):
        for level in range(len(near)):
            for c in range(colours):
                mask = orders[c][level]
                for offset in list(held[c]):
                    held[c][offset ^ mask] = permute(held[c][offset], mask, 0, sends)

    for mask in bits_below(feats):
        residue = residue + permute(residue, mask, 0, lambda f, d: f < mask)

    tile = min(256, chunk_width)
    gain = (norm_gain / token_total).reshape(full_width // tile, 1, tile)
    is_inside = (feat // share == part).astype(jnp.int32)
    hessian = None
    height = full_width // parts
    for position in range(1 << len(near)):
        for c in range(colours):
            offset = sum(orders[c][n] for n in range(len(near)) if position >> n & 1)
            block = ((feat % share) ^ offset) * colours + c
            place = jnp.stack([block, is_inside, part * share * colours + block]).astype(jnp.int32)
            hessian = gram_rows(
                place, inner[c][offset], outer[c][offset], scaled, gain, hessian, height
            )

    shift_terms = lax.dot_general(
        residue.astype(jnp.float32),
        inverse_factor,
        (((0,), (0,)), ((), ())),
        precision=lax.Precision.HIGHEST,
        preferred_element_type=jnp.float32,
    )
    updated = weights - shift_terms
    column_ids = lax.broadcasted_iota(jnp.int32, weights.shape, 1)
    padded_panel = jnp.pad(quantized, ((0, 0), (0, shard_width - panel_width)))
    updated = jnp.where((column_ids < panel_width) & (feat == 0), padded_panel, updated)
    return (hessian, updated)


def solution(mesh):
    placed = (P("dp", "feat"), P(), P("dp", "feat"), P(None, "feat"), P("dp"))
    return jax.shard_map(
        body,
        mesh=mesh,
        in_specs=placed,
        out_specs=(P("dp", "feat"), P("dp", "feat")),
        check_vma=False,
    )
```
